256 devices in a mesh: dish: 8 (over y, x_hi), blk: 32 (over x_lo, z, core).
Axes of the slice: x: 4 (x_hi: 2, x_lo: 2; x = x_hi * 2 + x_lo), y: 4, z: 8, core: 2. Of those that a mesh axis runs over, the one named last changes fastest.
Arguments:
- sky_data: float32 [8, 2048, 32768], P('dish', 'blk'), may hold values from -6 to 6
- eigenmodes: float32 [2048, 64], replicated, may hold values from -0.125 to 0.125
- noise_power: float32 [64, 32768], P('blk'), may hold values from 0.1 to 10
Outputs:
- cleaned: bfloat16 [8, 2048, 32768], P('dish', 'blk')
- mode_signal: float32 [8, 64, 32768], P('dish', 'blk')
The draws below stay inside these ranges and needn't reach their ends.
All inputs are finite; a program needn't handle non-finite values.
Results may differ from the reference program's by a relative error of at most 0.0028.
Values may be sent and summed in bfloat16 or wider, within the bound.
No kernel may reach another device: no remote copies, remote signals or barrier semaphores. Data moves between devices by JAX's collectives and lax.ppermute only.
A program may use at most 128 MiB of HBM per device.

```python
import math
import jax
import jax.numpy as jnp
from jax import lax

CH = 2048
MODES = 64
NT = 32768
DISHES = 8


def block_levels(key, shape, cuts, low, high):
    level, own = 1.0, jax.random.fold_in(key, 6)
    for axis_at, blocks in cuts:
        heights = jnp.exp(jax.random.uniform(jax.random.fold_in(own, axis_at), (blocks,), jnp.float32, low / len(cuts), high / len(cuts)))
        level = level * jnp.repeat(heights, shape[axis_at] // blocks).reshape([-1 if axis == axis_at else 1 for axis in range(len(shape))])
    return level


def bell_draw(rng, extent, deviation, most, pieces=(), held_as=jnp.bfloat16):
    factor_of = block_levels(rng, extent, pieces, -0.22, 0.18) if pieces else 1.0
    result = jax.random.normal(rng, extent, jnp.float32) * deviation * factor_of
    return jnp.minimum(jnp.maximum(result, -most), most).astype(held_as)


def setup_inputs(seed: int = 0) -> dict:
    key_list = jax.random.split(jax.random.key(seed), 4)
    sky_data = bell_draw(key_list[0], (DISHES, CH, NT), 1.0, 6.0, ((0, 8), (1, 32)), jnp.float32)
    eigenmodes = bell_draw(key_list[1], (CH, MODES), CH ** -0.5, 0.125, (), jnp.float32)
    noise_power = jnp.clip(jnp.exp(math.log(10.0) - 4.6051702 * jax.random.uniform(key_list[2], (MODES, NT), jnp.float32) ** block_levels(key_list[2], (MODES, NT), ((0, 32),), -0.2, 0.2)), 0.1, 10.0)
    return dict(sky_data=sky_data, eigenmodes=eigenmodes, noise_power=noise_power)


def reference(sky_data, eigenmodes, noise_power):
    def project(block):
        return jnp.dot(eigenmodes.T, block, precision=lax.Precision.HIGHEST, preferred_element_type=jnp.float32)

    amplitude = lax.map(project, sky_data)
    spectrum = jnp.fft.fft(amplitude, axis=-1)
    power = jnp.sum(spectrum.real * spectrum.real + spectrum.imag * spectrum.imag, axis=0) / (DISHES * NT)
    gain = power / (power + noise_power)
    mode_signal = jnp.fft.ifft(spectrum * gain[None], axis=-1).real.astype(jnp.float32)

    def remove(pair):
        block, signal = pair
        fitted = jnp.dot(eigenmodes, signal, precision=lax.Precision.HIGHEST, preferred_element_type=jnp.float32)
        return (block - fitted).astype(jnp.bfloat16)

    cleaned = lax.map(remove, (sky_data, mode_signal))
    return cleaned, mode_signal
```

```python
import math

import jax
import jax.numpy as jnp
import numpy as np
from jax import lax
from jax.experimental import pallas as pl
from jax.experimental.pallas import tpu as pltpu
from jax.sharding import Mesh
from jax.sharding import PartitionSpec as P


BF = jnp.bfloat16
F32 = jnp.float32
HI = lax.Precision.HIGHEST
STREAMS = 2
ROWS = 144
Q, LANES = 256, 128
LENGTH = Q * LANES
SPAN = LENGTH // STREAMS
BLOCK = min(8192, SPAN)
PIECE = 1024
SWAP = F32

ONWARD = [(2 * i + c, 2 * ((i + (1, -1)[c]) % 8) + c) for i in range(8) for c in range(2)]
FLIP = [(0, 1), (1, 0)]
VMEM = pl.BlockSpec(memory_space=pltpu.VMEM)


def params(mib):
    return pltpu.CompilerParams(vmem_limit_bytes=mib << 20)


def tables():
    k1 = np.arange(ROWS)[:, None]
    q = np.arange(Q)[None, :]
    p = np.arange(LANES)[None, :]
    a = 2 * np.pi * ((k1 * q) % Q) / Q
    col = np.concatenate([np.cos(a), -np.sin(a)], axis=0)
    b = 2 * np.pi * ((np.arange(LANES)[:, None] * p) % LANES) / LANES
    c, s = np.cos(b), np.sin(b)
    row = np.block([[c, -s], [s, c]])
    t = 2 * np.pi * ((k1 * p) % LENGTH) / LENGTH
    return [x.astype(np.float32) for x in (col, np.cos(t), np.sin(t), row)]


def mode_at(place, handler, sign, hop, core, side, stream):
    xl, z, c = place[1], place[2], place[3]
    h = c ^ handler
    far = z + hop * sign * (1 - 2 * h)
    return ((((xl ^ side) * 8 + (far & 7)) * 2 + (h ^ core)) << 1) + stream


def outward(place):
    r = lax.broadcasted_iota(jnp.int32, (64, 64), 0)
    m = lax.broadcasted_iota(jnp.int32, (64, 64), 1)
    slot = r & 31
    hop = jnp.where(slot < 24, 3 - (slot >> 3), jnp.where(slot < 28, 4, 0))
    core = jnp.where(slot < 24, (slot >> 2) & 1, 0)
    return (mode_at(place, r >> 5, 1, hop, core, (slot >> 1) & 1, slot & 1) == m).astype(F32)


def inward(place):
    r = lax.broadcasted_iota(jnp.int32, (64, 64), 0)
    m = lax.broadcasted_iota(jnp.int32, (64, 64), 1)
    piece = r >> 3
    hop = jnp.where(piece < 4, piece, jnp.where(piece < 7, piece - 3, 4))
    handler = jnp.where(piece < 7, (piece >= 4).astype(jnp.int32), (r >> 2) & 1)
    core = jnp.where(piece < 7, (r >> 2) & 1, 0)
    return (mode_at(place, handler, -1, hop, core, (r >> 1) & 1, r & 1) == m).astype(F32)


def split(x):
    high = x.astype(BF)
    return high, (x - high.astype(F32)).astype(BF)


def weights_kernel(place, modes, out_weight, in_weight):
    a = lax.broadcasted_iota(jnp.int32, (128, 64), 0)
    b = lax.broadcasted_iota(jnp.int32, (128, 64), 1)
    local = jnp.dot(modes[...], (a == b + 64 * place[3]).astype(F32), precision=HI, preferred_element_type=F32)
    high, low = split(jnp.dot(outward(place), local, precision=HI, preferred_element_type=F32))
    out_weight[...] = jnp.concatenate([high, low, high], axis=1)
    high, low = split(jnp.dot(inward(place), local, precision=HI, preferred_element_type=F32).T)
    in_weight[...] = jnp.concatenate([high, low], axis=1)


def weights(place, modes):
    return pl.pallas_call(
        weights_kernel,
        out_shape=[jax.ShapeDtypeStruct((64, 192), BF), jax.ShapeDtypeStruct((64, 128), BF)],
        grid_spec=pltpu.PrefetchScalarGridSpec(
            num_scalar_prefetch=1,
            grid=(1,),
            in_specs=[pl.BlockSpec((64, 128), lambda i, s: (0, s[0]))],
            out_specs=[VMEM, VMEM],
        ),
        compiler_params=params(8),
        name="weights",
    )(place, modes)


def project_kernel(weight, sky, own, oth):
    base = pl.program_id(0) * BLOCK

    @pl.loop(0, BLOCK // PIECE)
    def _(i):
        at = pl.multiple_of(i * PIECE, PIECE)
        to = pl.multiple_of(base + i * PIECE, PIECE)
        high, low = split(sky[:, pl.ds(at, PIECE)])
        out = jnp.dot(weight[...], jnp.concatenate([high, high, low], axis=0), preferred_element_type=F32)
        own[:, pl.ds(to, PIECE)] = out[:32]
        oth[:, pl.ds(to, PIECE)] = out[32:].astype(SWAP)


def project(weight, sky, stream):
    first = stream * SPAN // BLOCK
    return pl.pallas_call(
        project_kernel,
        out_shape=[jax.ShapeDtypeStruct((32, SPAN), d) for d in (F32, SWAP)],
        grid=(SPAN // BLOCK,),
        in_specs=[VMEM, pl.BlockSpec((64, BLOCK), lambda i: (0, first + i))],
        out_specs=[VMEM, VMEM],
        compiler_params=params(24),
        name=f"project{stream}",
    )(weight, sky)


def forward_kernel(*refs):
    totals, arrived = refs[:STREAMS], refs[STREAMS : 2 * STREAMS]
    col, tcos, tsin, row, real, imag, power = refs[2 * STREAMS :]
    parts = [t[...] + a[...].astype(F32) for t, a in zip(totals, arrived)]
    for m in range(2):
        x = jnp.concatenate([v[m : m + 1].reshape(SPAN // LANES, LANES) for v in parts], axis=0)
        inner = jnp.dot(col[...], x, precision=HI, preferred_element_type=F32)
        gr, gi = inner[:ROWS], inner[ROWS:]
        hr = gr * tcos[...] + gi * tsin[...]
        hi = gi * tcos[...] - gr * tsin[...]
        s = jnp.dot(jnp.concatenate([hr, hi], axis=1), row[...], precision=HI, preferred_element_type=F32)
        sr, si = s[:, :LANES], s[:, LANES:]
        real[m] = sr
        imag[m] = si
        power[m] = (sr * sr + si * si).astype(BF)


def forward(totals, arrived, *tabs):
    return pl.pallas_call(
        forward_kernel,
        out_shape=[jax.ShapeDtypeStruct((2, ROWS, LANES), d) for d in (F32, F32, BF)],
        compiler_params=params(12),
        name="forward",
    )(*totals, *arrived, *tabs)


def inverse_kernel(real, imag, here, there, noise, mirror, col, tcos, tsin, row, signal, *sent):
    k1 = lax.broadcasted_iota(jnp.int32, (ROWS, LANES), 0)
    once = jnp.where((k1 == 0) | (k1 == LANES), 1.0, jnp.where(k1 < LANES, 2.0, 0.0)) * (0.5 / LENGTH)
    for m in range(2):
        p = (here[m] + there[m].astype(F32)) * (1.0 / (8 * LENGTH))
        gain = once * (p / (p + noise[m]) + p / (p + mirror[m]))
        y = jnp.concatenate([real[m] * gain, imag[m] * gain], axis=1)
        u = lax.dot_general(y, row[...], (((1,), (1,)), ((), ())), precision=HI, preferred_element_type=F32)
        ur, ui = u[:, :LANES], u[:, LANES:]
        vr = ur * tcos[...] - ui * tsin[...]
        vi = ur * tsin[...] + ui * tcos[...]
        v = jnp.concatenate([vr, vi], axis=0)
        x = lax.dot_general(col[...], v, (((0,), (0,)), ((), ())), precision=HI, preferred_element_type=F32)
        line = x.reshape(1, LENGTH)
        signal[m : m + 1, :] = line
    for i, ref in enumerate(sent):
        ref[...] = signal[:, i * SPAN : (i + 1) * SPAN].astype(BF)


def inverse(*args):
    out = pl.pallas_call(
        inverse_kernel,
        out_shape=[jax.ShapeDtypeStruct((2, LENGTH), F32)] + [jax.ShapeDtypeStruct((2, SPAN), BF)] * STREAMS,
        compiler_params=params(12),
        name="inverse",
    )(*args)
    return out[0], out[1:]


def noise_kernel(noise, plain, mirror):
    for m in range(2):
        n = noise[m].T
        r = lax.broadcasted_iota(jnp.int32, (ROWS, Q), 0)
        k = lax.broadcasted_iota(jnp.int32, (ROWS, Q), 1)
        rows = (k == ((Q - r) & (Q - 1))).astype(F32)
        a = lax.broadcasted_iota(jnp.int32, (LANES, LANES), 0)
        b = lax.broadcasted_iota(jnp.int32, (LANES, LANES), 1)
        turned = jnp.dot(jnp.dot(rows, n, precision=HI), (a + b == LANES - 1).astype(F32), precision=HI)
        first = lax.broadcasted_iota(jnp.int32, (ROWS, LANES), 0) == 0
        plain[m] = n[:ROWS]
        mirror[m] = jnp.where(first, n[:ROWS], turned)


def noise_tables(noise):
    return pl.pallas_call(
        noise_kernel,
        out_shape=[jax.ShapeDtypeStruct((2, ROWS, LANES), F32)] * 2,
        compiler_params=params(12),
        name="noise",
    )(noise.reshape(2, LANES, Q))


def remove_kernel(weight, sky, *refs):
    pieces, cleaned = refs[: 9], refs[-1]
    base = pl.program_id(0) * BLOCK

    @pl.loop(0, BLOCK // PIECE)
    def _(i):
        at = pl.multiple_of(i * PIECE, PIECE)
        to = pl.multiple_of(base + i * PIECE, PIECE)
        signal = jnp.concatenate([p[:, pl.ds(to, PIECE)].astype(F32) for p in pieces], axis=0).astype(BF)
        fitted = jnp.dot(weight[...], jnp.concatenate([signal, signal], axis=0), preferred_element_type=F32)
        cleaned[:, pl.ds(at, PIECE)] = (sky[:, pl.ds(at, PIECE)] - fitted).astype(BF)


def remove(weight, sky, pieces, stream, cleaned):
    first = stream * SPAN // BLOCK
    block = pl.BlockSpec((64, BLOCK), lambda i: (0, first + i))
    before = [] if cleaned is None else [cleaned]
    return pl.pallas_call(
        remove_kernel,
        out_shape=jax.ShapeDtypeStruct((64, LENGTH), BF),
        grid=(SPAN // BLOCK,),
        in_specs=[VMEM, block] + [VMEM] * len(pieces) + [pl.BlockSpec(memory_space=pl.ANY)] * len(before),
        out_specs=block,
        input_output_aliases={2 + len(pieces): 0} if before else {},
        compiler_params=params(20),
        name=f"remove{stream}",
    )(weight, sky, *pieces, *before)


def onward(x):
    return lax.ppermute(x, ("z", "c"), ONWARD)


def reduced(own, oth):
    other = lax.ppermute(oth, "c", FLIP)

    def part(a, b):
        return own[a:b] + other[a:b].astype(F32)

    got = onward(part(24, 28).astype(BF)).astype(F32)
    got = onward(jnp.concatenate([part(0, 4) + got, part(4, 8)]).astype(BF)).astype(F32)
    got = onward((part(8, 16) + got).astype(BF)).astype(F32)
    got = onward((part(16, 24) + got).astype(BF))
    crossed = lax.ppermute(got[4:], "c", FLIP)
    total = part(28, 32) + got[:4].astype(F32) + crossed.astype(F32)
    return total[:2], lax.ppermute(total[2:].astype(BF), "xl", FLIP)


def over_dishes(power):
    here = power.astype(F32)
    for step in (1, 3, 2):
        here = here + lax.ppermute(power, "y", [(i, (i + step) % 4) for i in range(4)]).astype(F32)
    return here, lax.ppermute(here.astype(BF), "xh", FLIP)


def gathered(sent):
    pair = jnp.concatenate([sent, lax.ppermute(sent, "xl", FLIP)])
    quad = jnp.concatenate([pair, lax.ppermute(pair, "c", FLIP)])
    first = onward(quad)
    second = onward(first)
    third = onward(second)
    last = onward(third[:4])
    mine = [first, second, third]
    return [quad] + mine + [lax.ppermute(x, "c", FLIP) for x in mine] + [last, lax.ppermute(last, "c", FLIP)]


def body(sky_data, eigenmodes, noise_power):
    xl, z, c = (lax.axis_index(n) for n in ("xl", "z", "c"))
    place = jnp.stack([xl * 8 + z, xl, z, c]).astype(jnp.int32)
    sky = sky_data[0]
    tabs = tables()
    out_weight, in_weight = weights(place, eigenmodes.T)
    plain, mirror = noise_tables(noise_power)
    sums = [reduced(*project(out_weight, sky, i)) for i in range(STREAMS)]
    real, imag, power = forward([a for a, _ in sums], [b for _, b in sums], *tabs)
    here, there = over_dishes(power)
    signal, sent = inverse(real, imag, here, there, plain, mirror, *tabs)
    cleaned = None
    for i in range(STREAMS):
        cleaned = remove(in_weight, sky, gathered(sent[i]), i, cleaned)
    return cleaned[None], signal[None]


def solution(mesh):
    finer = Mesh(mesh.devices.reshape(4, 2, 2, 8, 2), ("y", "xh", "xl", "z", "c"))
    dish, blk = ("y", "xh"), ("xl", "z", "c")
    return jax.shard_map(
        body,
        mesh=finer,
        in_specs=(P(dish, blk, None), P(), P(blk, None)),
        out_specs=(P(dish, blk, None), P(dish, blk, None)),
        check_vma=False,
    )
```

```python
import functools

import jax
import jax.numpy as jnp
import numpy as np
from jax import lax
from jax.experimental import pallas as pl
from jax.experimental.pallas import tpu as pltpu
from jax.sharding import Mesh
from jax.sharding import PartitionSpec as P


BF = jnp.bfloat16
F32 = jnp.float32
HI = lax.Precision.HIGHEST
STRETCHES = 2
ROWS = 144
Q, LANES = 256, 128
LENGTH = Q * LANES
SPAN = LENGTH // STRETCHES
BLOCK = 4096
OUT = 8192
HBM = pltpu.HBM
PLIM = (40, 40)
ORDER = (0, 1)
PIECE = 4096
SWAP = F32

ONWARD = [(2 * i + c, 2 * ((i + (1, -1)[c]) % 8) + c) for i in range(8) for c in range(2)]
FLIP = [(0, 1), (1, 0)]
VMEM = pl.BlockSpec(memory_space=pltpu.VMEM)


def params(mib):
    return pltpu.CompilerParams(vmem_limit_bytes=mib << 20)


def tables():
    k1 = np.arange(ROWS)[:, None]
    q = np.arange(Q)[None, :]
    p = np.arange(LANES)[None, :]
    a = 2 * np.pi * ((k1 * q) % Q) / Q
    col = np.concatenate([np.cos(a), -np.sin(a)], axis=0)
    w = np.where((k1 == 0) | (k1 == 128), 1.0, np.where(k1 < 128, 2.0, 0.0)) / LENGTH
    back = np.concatenate([(np.cos(a) * w).T, (-np.sin(a) * w).T], axis=1)
    b = 2 * np.pi * ((np.arange(LANES)[:, None] * p) % LANES) / LANES
    c, s = np.cos(b), np.sin(b)
    row = np.block([[c, -s], [s, c]])
    t = 2 * np.pi * ((k1 * p) % LENGTH) / LENGTH
    twist = [np.cos(t).astype(np.float32), np.sin(t).astype(np.float32)]

    def halves(x):
        x = x.astype(np.float32)
        high = x.astype(BF)
        return [high, (x - high.astype(np.float32)).astype(BF)]

    return halves(col) + halves(row) + twist, halves(row.T) + halves(back) + twist


def mode_at(place, handler, sign, hop, core, side, stream):
    xl, z, c = place[1], place[2], place[3]
    h = c ^ handler
    far = z + hop * sign * (1 - 2 * h)
    return ((((xl ^ side) * 8 + (far & 7)) * 2 + (h ^ core)) << 1) + stream


def outward(place):
    r = lax.broadcasted_iota(jnp.int32, (64, 64), 0)
    m = lax.broadcasted_iota(jnp.int32, (64, 64), 1)
    group = r >> 3
    hop = jnp.where(group < 4, 4 - group, jnp.where(group < 7, 7 - group, 0))
    handler = jnp.where(group < 4, 0, jnp.where(group < 7, 1, (r >> 2) & 1))
    core = jnp.where(group < 7, (r >> 2) & 1, 0)
    return (mode_at(place, handler, 1, hop, core, (r >> 1) & 1, r & 1) == m).astype(F32)


def inward(place):
    r = lax.broadcasted_iota(jnp.int32, (64, 64), 0)
    m = lax.broadcasted_iota(jnp.int32, (64, 64), 1)
    piece = r >> 3
    hop = jnp.where(piece < 4, piece, jnp.where(piece < 7, piece - 3, 4))
    handler = jnp.where(piece < 7, (piece >= 4).astype(jnp.int32), (r >> 2) & 1)
    core = jnp.where(piece < 7, (r >> 2) & 1, 0)
    return (mode_at(place, handler, -1, hop, core, (r >> 1) & 1, r & 1) == m).astype(F32)


def split(x):
    high = x.astype(BF)
    return high, (x - high.astype(F32)).astype(BF)


def make_weights(place, modes, out_weight, in_weight):
    a = lax.broadcasted_iota(jnp.int32, (LANES, 64), 0)
    b = lax.broadcasted_iota(jnp.int32, (LANES, 64), 1)
    local = jnp.dot(modes[...], (a == b + 64 * place[3]).astype(F32), precision=HI, preferred_element_type=F32)
    high, low = split(jnp.dot(outward(place), local, precision=HI, preferred_element_type=F32))
    out_weight[...] = jnp.concatenate([high, low, high], axis=1)
    high, low = split(jnp.dot(inward(place), local, precision=HI, preferred_element_type=F32).T)
    in_weight[...] = jnp.concatenate([high, low], axis=1)


def project_kernel(stretch, place, *refs):
    if stretch == 0:
        modes_hbm, sky_hbm, out_weight, in_weight, sky, far, own, oth, modes, modes_sem, sems = refs
        at = pl.multiple_of(place[0] * LANES, LANES)
        fetch = pltpu.make_async_copy(modes_hbm.at[:, pl.ds(at, LANES)], modes, modes_sem)
        fetch.start()
    else:
        out_weight, sky_hbm, sky, far, own, oth, sems = refs
    copies = [
        pltpu.make_async_copy(
            sky_hbm.at[:, pl.ds(stretch * SPAN + i * BLOCK, BLOCK)], sky.at[:, pl.ds(i * BLOCK, BLOCK)], sems.at[i]
        )
        for i in range(SPAN // BLOCK)
    ]
    for copy in copies:
        copy.start()
    if stretch == 0:
        fetch.wait()
        make_weights(place, modes, out_weight, in_weight)
    for i, copy in enumerate(copies):
        copy.wait()

        @pl.loop(0, BLOCK // PIECE)
        def _(k):
            at = pl.ds(pl.multiple_of(i * BLOCK + k * PIECE, PIECE), PIECE)
            high, low = split(sky[:, at])
            out = jnp.dot(out_weight[...], jnp.concatenate([high, high, low], axis=0), preferred_element_type=F32)
            far[:, at] = out[:8].astype(BF)
            own[:24, at] = out[8:32]
            own[24:, at] = out[56:60]
            oth[:24, at] = out[32:56].astype(SWAP)
            oth[24:, at] = out[60:].astype(SWAP)


def project(place, weight, modes, sky, stretch):
    hbm = pl.BlockSpec(memory_space=HBM)
    shapes = [jax.ShapeDtypeStruct((64, SPAN), F32)]
    shapes += [jax.ShapeDtypeStruct((n, SPAN), d) for n, d in ((8, BF), (28, F32), (28, SWAP))]
    scratch = [pltpu.SemaphoreType.DMA((SPAN // BLOCK,))]
    if stretch == 0:
        shapes = [jax.ShapeDtypeStruct((64, 192), BF), jax.ShapeDtypeStruct((64, 128), BF)] + shapes
        scratch = [pltpu.VMEM((64, LANES), F32), pltpu.SemaphoreType.DMA] + scratch
    return pl.pallas_call(
        functools.partial(project_kernel, stretch),
        out_shape=shapes,
        in_specs=[pl.BlockSpec(memory_space=pltpu.SMEM)] + ([hbm, hbm] if stretch == 0 else [VMEM, hbm]),
        out_specs=[VMEM] * len(shapes),
        scratch_shapes=scratch,
        compiler_params=params(PLIM[stretch]),
        name=f"project{stretch}",
    )(place, modes if stretch == 0 else weight, sky)


def product(left, right):
    dot = functools.partial(jnp.dot, preferred_element_type=F32)
    return dot(left[0], right[0]) + (dot(left[0], right[1]) + dot(left[1], right[0]))


def forward_kernel(*refs):
    totals, arrived = refs[:STRETCHES], refs[STRETCHES : 2 * STRETCHES]
    colh, coll, rowh, rowl, tcos, tsin, real, imag, power = refs[2 * STRETCHES :]
    parts = [t[...] + a[...].astype(F32) for t, a in zip(totals, arrived)]
    grids = [
        jnp.concatenate([v[m : m + 1].reshape(SPAN // LANES, LANES) for v in parts], axis=0) for m in range(2)
    ]
    inner = product((colh[...], coll[...]), split(jnp.concatenate(grids, axis=1)))
    turned = []
    for m in range(2):
        gr, gi = inner[:ROWS, m * LANES : (m + 1) * LANES], inner[ROWS:, m * LANES : (m + 1) * LANES]
        turned.append(jnp.concatenate([gr * tcos[...] + gi * tsin[...], gi * tcos[...] - gr * tsin[...]], axis=1))
    s = product(split(jnp.concatenate(turned, axis=0)), (rowh[...], rowl[...]))
    for m in range(2):
        sr, si = s[m * ROWS : (m + 1) * ROWS, :LANES], s[m * ROWS : (m + 1) * ROWS, LANES:]
        real[m] = sr
        imag[m] = si
        power[m] = (sr * sr + si * si).astype(BF)


def forward(totals, arrived, tabs):
    return pl.pallas_call(
        forward_kernel,
        out_shape=[jax.ShapeDtypeStruct((2, ROWS, LANES), d) for d in (F32, F32, BF)],
        compiler_params=params(12),
        name="forward",
    )(*totals, *arrived, *tabs)


def inverse_kernel(real, imag, here, there, noise, mirror, rowh, rowl, backh, backl, tcos, tsin, signal, *sent):
    held = []
    for m in range(2):
        p = (here[m] + there[m].astype(F32)) * (1.0 / (8 * LENGTH))
        gain = 0.5 * (p / (p + noise[m]) + p / (p + mirror[m]))
        held.append(jnp.concatenate([real[m] * gain, imag[m] * gain], axis=1))
    u = product(split(jnp.concatenate(held, axis=0)), (rowh[...], rowl[...]))
    turned = []
    for m in range(2):
        ur, ui = u[m * ROWS : (m + 1) * ROWS, :LANES], u[m * ROWS : (m + 1) * ROWS, LANES:]
        turned.append(jnp.concatenate([ur * tcos[...] - ui * tsin[...], ur * tsin[...] + ui * tcos[...]], axis=0))
    x = product((backh[...], backl[...]), split(jnp.concatenate(turned, axis=1)))
    for m in range(2):
        signal[m : m + 1, :] = x[:, m * LANES : (m + 1) * LANES].reshape(1, LENGTH)
    for i, ref in enumerate(sent):
        ref[...] = signal[:, i * SPAN : (i + 1) * SPAN].astype(BF)


def inverse(*args):
    out = pl.pallas_call(
        inverse_kernel,
        out_shape=[jax.ShapeDtypeStruct((2, LENGTH), F32)] + [jax.ShapeDtypeStruct((2, SPAN), BF)] * STRETCHES,
        compiler_params=params(12),
        name="inverse",
    )(*args)
    return out[0], out[1:]


def noise_kernel(noise, plain, mirror):
    for m in range(2):
        n = noise[m].T
        r = lax.broadcasted_iota(jnp.int32, (ROWS, Q), 0)
        k = lax.broadcasted_iota(jnp.int32, (ROWS, Q), 1)
        rows = (k == ((Q - r) & (Q - 1))).astype(F32)
        a = lax.broadcasted_iota(jnp.int32, (LANES, LANES), 0)
        b = lax.broadcasted_iota(jnp.int32, (LANES, LANES), 1)
        turned = jnp.dot(jnp.dot(rows, n, precision=HI), (a + b == LANES - 1).astype(F32), precision=HI)
        first = lax.broadcasted_iota(jnp.int32, (ROWS, LANES), 0) == 0
        plain[m] = n[:ROWS]
        mirror[m] = jnp.where(first, n[:ROWS], turned)


def noise_tables(noise):
    return pl.pallas_call(
        noise_kernel,
        out_shape=[jax.ShapeDtypeStruct((2, ROWS, LANES), F32)] * 2,
        compiler_params=params(12),
        name="noise",
    )(noise.reshape(2, LANES, Q))


def remove_kernel(weight, sky, *refs):
    pieces, cleaned = refs[:9], refs[-1]
    base = pl.program_id(0) * OUT

    @pl.loop(0, OUT // PIECE)
    def _(i):
        at = pl.multiple_of(i * PIECE, PIECE)
        to = pl.ds(pl.multiple_of(base + i * PIECE, PIECE), PIECE)
        signal = jnp.concatenate([p[:, to].astype(F32) for p in pieces], axis=0).astype(BF)
        fitted = jnp.dot(weight[...], jnp.concatenate([signal, signal], axis=0), preferred_element_type=F32)
        cleaned[:, pl.ds(at, PIECE)] = (sky[:, to] - fitted).astype(BF)


def remove(weight, sky, pieces, stretch, cleaned):
    first = stretch * SPAN // OUT
    before = [] if cleaned is None else [cleaned]
    return pl.pallas_call(
        remove_kernel,
        out_shape=jax.ShapeDtypeStruct((64, LENGTH), BF),
        grid=(SPAN // OUT,),
        in_specs=[VMEM] * (2 + len(pieces)) + [pl.BlockSpec(memory_space=pl.ANY)] * len(before),
        out_specs=pl.BlockSpec((64, OUT), lambda i: (0, first + i)),
        input_output_aliases={2 + len(pieces): 0} if before else {},
        compiler_params=params(16),
        name=f"remove{stretch}",
    )(weight, sky, *pieces, *before)


def onward(x):
    return lax.ppermute(x, ("z", "c"), ONWARD)


def reduced(far, own, oth):
    other = lax.ppermute(oth, "c", FLIP)

    def part(a, b):
        return own[a:b] + other[a:b].astype(F32)

    got = onward(far)
    for a in (0, 8, 16):
        got = onward((part(a, a + 8) + got.astype(F32)).astype(BF))
    crossed = lax.ppermute(got[4:], "c", FLIP)
    total = part(24, 28) + got[:4].astype(F32) + crossed.astype(F32)
    return total[:2], lax.ppermute(total[2:].astype(BF), "xl", FLIP)


def over_dishes(power):
    here = power.astype(F32)
    for step in (1, 3, 2):
        here = here + lax.ppermute(power, "y", [(i, (i + step) % 4) for i in range(4)]).astype(F32)
    return here, lax.ppermute(here.astype(BF), "xh", FLIP)


def gathered(sent):
    pair = jnp.concatenate([sent, lax.ppermute(sent, "xl", FLIP)])
    quad = jnp.concatenate([pair, lax.ppermute(pair, "c", FLIP)])
    first = onward(quad)
    second = onward(first)
    third = onward(second)
    last = onward(third[:4])
    mine = [first, second, third]
    return [quad] + mine + [lax.ppermute(x, "c", FLIP) for x in mine] + [last, lax.ppermute(last, "c", FLIP)]


def body(sky_data, eigenmodes, noise_power):
    xl, z, c = (lax.axis_index(n) for n in ("xl", "z", "c"))
    place = jnp.stack([xl * 8 + z, xl, z, c]).astype(jnp.int32)
    sky = sky_data[0]
    ahead, back = tables()
    plain, mirror = noise_tables(noise_power)
    out_weight, in_weight, *parts0 = project(place, None, eigenmodes.T, sky, 0)
    parts = [parts0, project(place, out_weight, None, sky, 1)]
    sums = [reduced(*p[1:]) for p in parts]
    real, imag, power = forward([a for a, _ in sums], [b for _, b in sums], ahead)
    here, there = over_dishes(power)
    signal, sent = inverse(real, imag, here, there, plain, mirror, *back)
    cleaned = None
    for i in ORDER:
        cleaned = remove(in_weight, parts[i][0], gathered(sent[i]), i, cleaned)
    return cleaned[None], signal[None]


def solution(mesh):
    finer = Mesh(mesh.devices.reshape(4, 2, 2, 8, 2), ("y", "xh", "xl", "z", "c"))
    dish, blk = ("y", "xh"), ("xl", "z", "c")
    return jax.shard_map(
        body,
        mesh=finer,
        in_specs=(P(dish, blk, None), P(), P(blk, None)),
        out_specs=(P(dish, blk, None), P(dish, blk, None)),
        check_vma=False,
    )
```

```python
import functools

import jax
import jax.numpy as jnp
import numpy as np
from jax import lax
from jax.experimental import pallas as pl
from jax.experimental.pallas import tpu as pltpu
from jax.sharding import Mesh
from jax.sharding import PartitionSpec as P


BF = jnp.bfloat16
F32 = jnp.float32
HI = lax.Precision.HIGHEST
STRETCHES = 2
ROWS = 144
Q, LANES = 256, 128
LENGTH = Q * LANES
SPAN = LENGTH // STRETCHES
BLOCK = 4096
OUT = 8192
HBM = pltpu.HBM
PLIM = (40, 40)
PIECE = 4096

ONWARD = [(2 * i + c, 2 * ((i + (1, -1)[c]) % 8) + c) for i in range(8) for c in range(2)]
FLIP = [(0, 1), (1, 0)]
DIAGONAL = [(16 * x + a, 16 * (1 - x) + b) for x in range(2) for a, b in ONWARD]
VMEM = pl.BlockSpec(memory_space=pltpu.VMEM)


def params(mib):
    return pltpu.CompilerParams(vmem_limit_bytes=mib << 20)


def tables():
    k1 = np.arange(ROWS)[:, None]
    q = np.arange(Q)[None, :]
    p = np.arange(LANES)[None, :]
    a = 2 * np.pi * ((k1 * q) % Q) / Q
    col = np.concatenate([np.cos(a), -np.sin(a)], axis=0)
    w = np.where((k1 == 0) | (k1 == 128), 1.0, np.where(k1 < 128, 2.0, 0.0)) / LENGTH
    back = np.concatenate([(np.cos(a) * w).T, (-np.sin(a) * w).T], axis=1)
    b = 2 * np.pi * ((np.arange(LANES)[:, None] * p) % LANES) / LANES
    c, s = np.cos(b), np.sin(b)
    row = np.block([[c, -s], [s, c]])
    t = 2 * np.pi * ((k1 * p) % LENGTH) / LENGTH
    twist = [np.cos(t).astype(np.float32), np.sin(t).astype(np.float32)]

    def halves(x):
        x = x.astype(np.float32)
        high = x.astype(BF)
        return [high, (x - high.astype(np.float32)).astype(BF)]

    return halves(col) + halves(row) + twist, halves(row.T) + halves(back) + twist


def mode_at(place, handler, sign, hop, core, side, stream):
    xl, z, c = place[1], place[2], place[3]
    h = c ^ handler
    far = z + hop * sign * (1 - 2 * h)
    return ((((xl ^ side) * 8 + (far & 7)) * 2 + (h ^ core)) << 1) + stream


def outward(place):
    r = lax.broadcasted_iota(jnp.int32, (64, 64), 0)
    m = lax.broadcasted_iota(jnp.int32, (64, 64), 1)
    group = r >> 3
    hop = jnp.where(group < 4, 4 - group, jnp.where(group < 7, 7 - group, 0))
    handler = jnp.where(group < 4, 0, jnp.where(group < 7, 1, (r >> 2) & 1))
    core = jnp.where(group < 7, (r >> 1) & 1, 0)
    side = jnp.where(group < 7, (r >> 2) & 1, (r >> 1) & 1)
    return (mode_at(place, handler, 1, hop, core, side, r & 1) == m).astype(F32)


def inward(place):
    r = lax.broadcasted_iota(jnp.int32, (64, 64), 0)
    m = lax.broadcasted_iota(jnp.int32, (64, 64), 1)
    piece = (r >> 2) & 7
    hop = jnp.where(piece < 4, piece, jnp.where(piece < 7, piece - 3, 4))
    handler = jnp.where(piece < 7, (piece >= 4).astype(jnp.int32), (r >> 1) & 1)
    core = jnp.where(piece < 7, (r >> 1) & 1, 0)
    return (mode_at(place, handler, -1, hop, core, r >> 5, r & 1) == m).astype(F32)


def split(x):
    high = x.astype(BF)
    return high, (x - high.astype(F32)).astype(BF)


def make_weights(place, modes, out_weight, in_weight):
    a = lax.broadcasted_iota(jnp.int32, (LANES, 64), 0)
    b = lax.broadcasted_iota(jnp.int32, (LANES, 64), 1)
    local = jnp.dot(modes[...], (a == b + 64 * place[3]).astype(F32), precision=HI, preferred_element_type=F32)
    high, low = split(jnp.dot(outward(place), local, precision=HI, preferred_element_type=F32))
    out_weight[...] = jnp.concatenate([high, low, high], axis=1)
    high, low = split(jnp.dot(inward(place), local, precision=HI, preferred_element_type=F32).T)
    in_weight[...] = jnp.concatenate([high, low], axis=1)


def project_kernel(stretch, place, *refs):
    if stretch == 0:
        modes_hbm, sky_hbm, out_weight, in_weight, sky, far, own, oth, modes, modes_sem, sems = refs
        at = pl.multiple_of(place[0] * LANES, LANES)
        fetch = pltpu.make_async_copy(modes_hbm.at[:, pl.ds(at, LANES)], modes, modes_sem)
        fetch.start()
    else:
        out_weight, sky_hbm, sky, far, own, oth, sems = refs
    copies = [
        pltpu.make_async_copy(
            sky_hbm.at[:, pl.ds(stretch * SPAN + i * BLOCK, BLOCK)], sky.at[:, pl.ds(i * BLOCK, BLOCK)], sems.at[i]
        )
        for i in range(SPAN // BLOCK)
    ]
    for copy in copies:
        copy.start()
    if stretch == 0:
        fetch.wait()
        make_weights(place, modes, out_weight, in_weight)
    for i, copy in enumerate(copies):
        copy.wait()

        @pl.loop(0, BLOCK // PIECE)
        def _(k):
            at = pl.ds(pl.multiple_of(i * BLOCK + k * PIECE, PIECE), PIECE)
            high, low = split(sky[:, at])
            out = jnp.dot(out_weight[...], jnp.concatenate([high, high, low], axis=0), preferred_element_type=F32)
            far[:, at] = out[:8].astype(BF)
            own[:24, at] = out[8:32]
            own[24:, at] = out[56:60]
            oth[:24, at] = out[32:56].astype(F32)
            oth[24:, at] = out[60:].astype(F32)


def project(place, weight, modes, sky, stretch):
    hbm = pl.BlockSpec(memory_space=HBM)
    shapes = [jax.ShapeDtypeStruct((64, SPAN), F32)]
    shapes += [jax.ShapeDtypeStruct((n, SPAN), d) for n, d in ((8, BF), (28, F32), (28, F32))]
    scratch = [pltpu.SemaphoreType.DMA((SPAN // BLOCK,))]
    if stretch == 0:
        shapes = [jax.ShapeDtypeStruct((64, 192), BF), jax.ShapeDtypeStruct((64, 128), BF)] + shapes
        scratch = [pltpu.VMEM((64, LANES), F32), pltpu.SemaphoreType.DMA] + scratch
    return pl.pallas_call(
        functools.partial(project_kernel, stretch),
        out_shape=shapes,
        in_specs=[pl.BlockSpec(memory_space=pltpu.SMEM)] + ([hbm, hbm] if stretch == 0 else [VMEM, hbm]),
        out_specs=[VMEM] * len(shapes),
        scratch_shapes=scratch,
        compiler_params=params(PLIM[stretch]),
    )(place, modes if stretch == 0 else weight, sky)


def product(left, right):
    dot = functools.partial(jnp.dot, preferred_element_type=F32)
    return dot(left[0], right[0]) + (dot(left[0], right[1]) + dot(left[1], right[0]))


def forward_kernel(*refs):
    totals, crossed = refs[:STRETCHES], refs[STRETCHES : 2 * STRETCHES]
    colh, coll, rowh, rowl, tcos, tsin, real, imag, power = refs[2 * STRETCHES :]
    parts = [t[...] + c[...] for t, c in zip(totals, crossed)]
    grids = [
        jnp.concatenate([v[m : m + 1].reshape(SPAN // LANES, LANES) for v in parts], axis=0) for m in range(2)
    ]
    inner = product((colh[...], coll[...]), split(jnp.concatenate(grids, axis=1)))
    turned = []
    for m in range(2):
        gr, gi = inner[:ROWS, m * LANES : (m + 1) * LANES], inner[ROWS:, m * LANES : (m + 1) * LANES]
        turned.append(jnp.concatenate([gr * tcos[...] + gi * tsin[...], gi * tcos[...] - gr * tsin[...]], axis=1))
    s = product(split(jnp.concatenate(turned, axis=0)), (rowh[...], rowl[...]))
    for m in range(2):
        sr, si = s[m * ROWS : (m + 1) * ROWS, :LANES], s[m * ROWS : (m + 1) * ROWS, LANES:]
        real[m] = sr
        imag[m] = si
        power[m] = (sr * sr + si * si).astype(BF)


def forward(totals, crossed, tabs):
    return pl.pallas_call(
        forward_kernel,
        out_shape=[jax.ShapeDtypeStruct((2, ROWS, LANES), d) for d in (F32, F32, BF)],
        compiler_params=params(12),
        name="forward",
    )(*totals, *crossed, *tabs)


def inverse_kernel(real, imag, here, there, noise, mirror, rowh, rowl, backh, backl, tcos, tsin, signal, sent):
    held = []
    for m in range(2):
        p = (here[m] + there[m].astype(F32)) * (1.0 / (8 * LENGTH))
        gain = 0.5 * (p / (p + noise[m]) + p / (p + mirror[m]))
        held.append(jnp.concatenate([real[m] * gain, imag[m] * gain], axis=1))
    u = product(split(jnp.concatenate(held, axis=0)), (rowh[...], rowl[...]))
    turned = []
    for m in range(2):
        ur, ui = u[m * ROWS : (m + 1) * ROWS, :LANES], u[m * ROWS : (m + 1) * ROWS, LANES:]
        turned.append(jnp.concatenate([ur * tcos[...] - ui * tsin[...], ur * tsin[...] + ui * tcos[...]], axis=0))
    x = product((backh[...], backl[...]), split(jnp.concatenate(turned, axis=1)))
    for m in range(2):
        signal[m : m + 1, :] = x[:, m * LANES : (m + 1) * LANES].reshape(1, LENGTH)
    sent[...] = signal[...].astype(BF)


def inverse(*args):
    return pl.pallas_call(
        inverse_kernel,
        out_shape=[jax.ShapeDtypeStruct((2, LENGTH), d) for d in (F32, BF)],
        compiler_params=params(12),
        name="inverse",
    )(*args)


def noise_kernel(noise, plain, mirror):
    for m in range(2):
        n = noise[m].T
        r = lax.broadcasted_iota(jnp.int32, (ROWS, Q), 0)
        k = lax.broadcasted_iota(jnp.int32, (ROWS, Q), 1)
        rows = (k == ((Q - r) & (Q - 1))).astype(F32)
        a = lax.broadcasted_iota(jnp.int32, (LANES, LANES), 0)
        b = lax.broadcasted_iota(jnp.int32, (LANES, LANES), 1)
        turned = jnp.dot(jnp.dot(rows, n, precision=HI), (a + b == LANES - 1).astype(F32), precision=HI)
        first = lax.broadcasted_iota(jnp.int32, (ROWS, LANES), 0) == 0
        plain[m] = n[:ROWS]
        mirror[m] = jnp.where(first, n[:ROWS], turned)


def noise_tables(noise):
    return pl.pallas_call(
        noise_kernel,
        out_shape=[jax.ShapeDtypeStruct((2, ROWS, LANES), F32)] * 2,
        compiler_params=params(12),
        name="noise",
    )(noise.reshape(2, LANES, Q))


def remove_kernel(weight, sky0, sky1, *refs):
    pieces, cleaned = refs[:-1], refs[-1]
    base = pl.program_id(0) * OUT

    @pl.loop(0, OUT // PIECE)
    def _(i):
        at = pl.multiple_of(i * PIECE, PIECE)
        to = pl.ds(pl.multiple_of(base + i * PIECE, PIECE), PIECE)
        signal = jnp.concatenate([p[:, to].astype(F32) for p in pieces], axis=0).astype(BF)
        fitted = jnp.dot(weight[...], jnp.concatenate([signal, signal], axis=0), preferred_element_type=F32)
        here = pl.ds(pl.multiple_of(lax.rem(base, SPAN) + i * PIECE, PIECE), PIECE)

        @pl.when(base < SPAN)
        def _():
            cleaned[:, pl.ds(at, PIECE)] = (sky0[:, here] - fitted).astype(BF)

        @pl.when(base >= SPAN)
        def _():
            cleaned[:, pl.ds(at, PIECE)] = (sky1[:, here] - fitted).astype(BF)


def remove(weight, skies, pieces):
    return pl.pallas_call(
        remove_kernel,
        out_shape=jax.ShapeDtypeStruct((64, LENGTH), BF),
        grid=(LENGTH // OUT,),
        in_specs=[VMEM] * (3 + len(pieces)),
        out_specs=pl.BlockSpec((64, OUT), lambda i: (0, i)),
        compiler_params=params(16),
        name="remove",
    )(weight, *skies, *pieces)


def onward(x):
    return lax.ppermute(x, ("z", "c"), ONWARD)


def diagonal(x):
    return lax.ppermute(x, ("xl", "z", "c"), DIAGONAL)


def flip(x, axis):
    return lax.ppermute(x, axis, FLIP)


def reduced(far, own, oth):
    other = flip(oth, "c")
    got = onward(far)
    for hop in range(3):
        a = 8 * hop
        got = (own[a : a + 8] + other[a : a + 8] + got.astype(F32)).astype(BF)
        if hop < 2:
            got = onward(got)
    across = diagonal(got[4:])
    near = onward(got[:4])
    both = near.astype(F32) + across.astype(F32)
    return own[24:] + other[24:], both[:2], flip(both[2:], "c")


def over_dishes(power):
    here = power.astype(F32)
    for step in (1, 3, 2):
        here = here + lax.ppermute(power, "y", [(i, (i + step) % 4) for i in range(4)]).astype(F32)
    return here, lax.ppermute(here.astype(BF), "xh", FLIP)


def gathered(quad, first):
    second = onward(first)
    third = onward(second)
    last = onward(third[:2])
    mine = [first, second, third]
    theirs = [flip(x, "c") for x in mine]
    return [quad] + mine + theirs + [last, flip(last, "c")]


def work(sky_data, eigenmodes, noise_power):
    xl, z, c = (lax.axis_index(n) for n in ("xl", "z", "c"))
    place = jnp.stack([xl * 8 + z, xl, z, c]).astype(jnp.int32)
    sky = sky_data[0]
    ahead, back = tables()
    plain, mirror = noise_tables(noise_power)
    out_weight, in_weight, *parts0 = project(place, None, eigenmodes.T, sky, 0)
    parts = [parts0, project(place, out_weight, None, sky, 1)]
    sums = [reduced(*p[1:]) for p in parts]
    beside = flip(jnp.concatenate([h[2:] for h, _, _ in sums], axis=1).astype(BF), "xl")
    totals = [
        home[:2] + both + beside[:, i * SPAN : (i + 1) * SPAN].astype(F32) for i, (home, both, _) in enumerate(sums)
    ]
    real, imag, power = forward(totals, [c for _, _, c in sums], ahead)
    here, there = over_dishes(power)
    signal, sent = inverse(real, imag, here, there, plain, mirror, *back)
    quad = jnp.concatenate([sent, flip(sent, "c")])
    across = gathered(flip(quad, "xl"), diagonal(quad))
    near = gathered(quad, onward(quad))
    cleaned = remove(in_weight, [p[0] for p in parts], near + across)
    return cleaned[None], signal[None]


def solution(mesh):
    finer = Mesh(mesh.devices.reshape(4, 2, 2, 8, 2), ("y", "xh", "xl", "z", "c"))
    dish, blk = ("y", "xh"), ("xl", "z", "c")
    return jax.shard_map(
        work,
        mesh=finer,
        in_specs=(P(dish, blk, None), P(), P(blk, None)),
        out_specs=(P(dish, blk, None), P(dish, blk, None)),
        check_vma=False,
    )
```

```python
import functools

import jax
import jax.numpy as jnp
import numpy as np
from jax import lax
from jax.experimental import pallas as pl
from jax.experimental.pallas import tpu as pltpu
from jax.sharding import Mesh
from jax.sharding import PartitionSpec as P


BF = jnp.bfloat16
F32 = jnp.float32
HI = lax.Precision.HIGHEST
STRETCHES = 2
ROWS = 136
Q, LANES = 256, 128
LENGTH = Q * LANES
SPANS = (16384, 16384)
FIRSTS = (0, 16384)
BLOCK = 4096
HBM = pltpu.HBM
PLIM = (40, 40)
PIECE = 4096

ONWARD = [(2 * i + c, 2 * ((i + (1, -1)[c]) % 8) + c) for i in range(8) for c in range(2)]
FLIP = [(0, 1), (1, 0)]
DIAGONAL = [(16 * x + a, 16 * (1 - x) + b) for x in range(2) for a, b in ONWARD]
VMEM = pl.BlockSpec(memory_space=pltpu.VMEM)


def params(mib):
    return pltpu.CompilerParams(vmem_limit_bytes=mib << 20)


def tables():
    k1 = np.arange(ROWS)[:, None]
    q = np.arange(Q)[None, :]
    p = np.arange(LANES)[None, :]
    a = 2 * np.pi * ((k1 * q) % Q) / Q
    col = np.concatenate([np.cos(a), -np.sin(a)], axis=0)
    w = np.where((k1 == 0) | (k1 == 128), 1.0, np.where(k1 < 128, 2.0, 0.0)) / LENGTH
    back = np.concatenate([(np.cos(a) * w).T, (-np.sin(a) * w).T], axis=1)
    b = 2 * np.pi * ((np.arange(LANES)[:, None] * p) % LANES) / LANES
    c, s = np.cos(b), np.sin(b)
    row = np.block([[c, -s], [s, c]])
    t = 2 * np.pi * ((k1 * p) % LENGTH) / LENGTH
    twist = [np.cos(t).astype(np.float32), np.sin(t).astype(np.float32)]

    def halves(x):
        x = x.astype(np.float32)
        high = x.astype(BF)
        return [high, (x - high.astype(np.float32)).astype(BF)]

    return halves(col) + halves(row) + twist, halves(row.T) + halves(back) + twist


def mode_at(place, handler, sign, hop, core, side, stream):
    xl, z, c = place[1], place[2], place[3]
    h = c ^ handler
    far = z + hop * sign * (1 - 2 * h)
    return ((((xl ^ side) * 8 + (far & 7)) * 2 + (h ^ core)) << 1) + stream


def outward(place):
    r = lax.broadcasted_iota(jnp.int32, (64, 64), 0)
    m = lax.broadcasted_iota(jnp.int32, (64, 64), 1)
    group = r >> 3
    hop = jnp.where(group < 4, 4 - group, jnp.where(group < 7, 7 - group, 0))
    handler = jnp.where(group < 4, 0, jnp.where(group < 7, 1, (r >> 2) & 1))
    core = jnp.where(group < 7, (r >> 1) & 1, 0)
    side = jnp.where(group < 7, (r >> 2) & 1, (r >> 1) & 1)
    return (mode_at(place, handler, 1, hop, core, side, r & 1) == m).astype(F32)


def inward(place):
    r = lax.broadcasted_iota(jnp.int32, (64, 64), 0)
    m = lax.broadcasted_iota(jnp.int32, (64, 64), 1)
    piece = (r >> 2) & 7
    hop = jnp.where(piece < 4, piece, jnp.where(piece < 7, piece - 3, 4))
    handler = jnp.where(piece < 7, (piece >= 4).astype(jnp.int32), (r >> 1) & 1)
    core = jnp.where(piece < 7, (r >> 1) & 1, 0)
    return (mode_at(place, handler, -1, hop, core, r >> 5, r & 1) == m).astype(F32)


def split(x):
    high = x.astype(BF)
    return high, (x - high.astype(F32)).astype(BF)


def local_modes(place, modes):
    return jnp.where(place[3] == 0, modes[:, :64], modes[:, 64:])


def project_kernel(stretch, place, *refs):
    if stretch == 0:
        modes_hbm, sky_hbm, out_weight, modes, sky, far, own, oth, modes_sem, sems = refs
        at = pl.multiple_of(place[0] * LANES, LANES)
        fetch = pltpu.make_async_copy(modes_hbm.at[:, pl.ds(at, LANES)], modes, modes_sem)
        fetch.start()
    else:
        out_weight, sky_hbm, sky, far, own, oth, sems = refs
    copies = [
        pltpu.make_async_copy(
            sky_hbm.at[:, pl.ds(FIRSTS[stretch] + i * BLOCK, BLOCK)], sky.at[:, pl.ds(i * BLOCK, BLOCK)], sems.at[i]
        )
        for i in range(SPANS[stretch] // BLOCK)
    ]
    for copy in copies:
        copy.start()
    if stretch == 0:
        fetch.wait()
        high, low = split(jnp.dot(outward(place), local_modes(place, modes), precision=HI, preferred_element_type=F32))
        out_weight[...] = jnp.concatenate([high, low, high], axis=1)
    for i, copy in enumerate(copies):
        copy.wait()

        @pl.loop(0, BLOCK // PIECE)
        def _(k):
            at = pl.ds(pl.multiple_of(i * BLOCK + k * PIECE, PIECE), PIECE)
            high, low = split(sky[:, at])
            out = jnp.dot(out_weight[...], jnp.concatenate([high, high, low], axis=0), preferred_element_type=F32)
            far[:, at] = out[:8].astype(BF)
            own[:24, at] = out[8:32]
            own[24:, at] = out[56:60]
            oth[:24, at] = out[32:56].astype(F32)
            oth[24:, at] = out[60:].astype(F32)


def project(place, weight, modes, sky, stretch):
    hbm = pl.BlockSpec(memory_space=HBM)
    shapes = [jax.ShapeDtypeStruct((64, SPANS[stretch]), F32)]
    shapes += [jax.ShapeDtypeStruct((n, SPANS[stretch]), d) for n, d in ((8, BF), (28, F32), (28, F32))]
    scratch = [pltpu.SemaphoreType.DMA((SPANS[stretch] // BLOCK,))]
    if stretch == 0:
        shapes = [jax.ShapeDtypeStruct((64, 192), BF), jax.ShapeDtypeStruct((64, LANES), F32)] + shapes
        scratch = [pltpu.SemaphoreType.DMA] + scratch
    return pl.pallas_call(
        functools.partial(project_kernel, stretch),
        out_shape=shapes,
        in_specs=[pl.BlockSpec(memory_space=pltpu.SMEM)] + ([hbm, hbm] if stretch == 0 else [VMEM, hbm]),
        out_specs=[VMEM] * len(shapes),
        scratch_shapes=scratch,
        compiler_params=params(PLIM[stretch]),
    )(place, modes if stretch == 0 else weight, sky)


def product(left, right):
    dot = functools.partial(jnp.dot, preferred_element_type=F32)
    return dot(left[0], right[0]) + (dot(left[0], right[1]) + dot(left[1], right[0]))


def forward_kernel(*refs):
    totals, crossed = refs[:STRETCHES], refs[STRETCHES : 2 * STRETCHES]
    colh, coll, rowh, rowl, tcos, tsin, real, imag, power = refs[2 * STRETCHES :]
    parts = [t[...] + c[...] for t, c in zip(totals, crossed)]
    grids = [
        jnp.concatenate([v[m : m + 1].reshape(v.shape[1] // LANES, LANES) for v in parts], axis=0) for m in range(2)
    ]
    inner = product((colh[...], coll[...]), split(jnp.concatenate(grids, axis=1)))
    turned = []
    for m in range(2):
        gr, gi = inner[:ROWS, m * LANES : (m + 1) * LANES], inner[ROWS:, m * LANES : (m + 1) * LANES]
        turned.append(jnp.concatenate([gr * tcos[...] + gi * tsin[...], gi * tcos[...] - gr * tsin[...]], axis=1))
    s = product(split(jnp.concatenate(turned, axis=0)), (rowh[...], rowl[...]))
    for m in range(2):
        sr, si = s[m * ROWS : (m + 1) * ROWS, :LANES], s[m * ROWS : (m + 1) * ROWS, LANES:]
        real[m] = sr
        imag[m] = si
        power[m] = (sr * sr + si * si).astype(BF)


def forward(totals, crossed, tabs):
    return pl.pallas_call(
        forward_kernel,
        out_shape=[jax.ShapeDtypeStruct((2, ROWS, LANES), d) for d in (F32, F32, BF)],
        compiler_params=params(12),
        name="forward",
    )(*totals, *crossed, *tabs)


def inverse_kernel(real, imag, here, there, noise, mirror, rowh, rowl, backh, backl, tcos, tsin, signal, sent):
    held = []
    for m in range(2):
        p = (here[m] + there[m].astype(F32)) * (1.0 / (8 * LENGTH))
        gain = 0.5 * (p / (p + noise[m]) + p / (p + mirror[m]))
        held.append(jnp.concatenate([real[m] * gain, imag[m] * gain], axis=1))
    u = product(split(jnp.concatenate(held, axis=0)), (rowh[...], rowl[...]))
    turned = []
    for m in range(2):
        ur, ui = u[m * ROWS : (m + 1) * ROWS, :LANES], u[m * ROWS : (m + 1) * ROWS, LANES:]
        turned.append(jnp.concatenate([ur * tcos[...] - ui * tsin[...], ur * tsin[...] + ui * tcos[...]], axis=0))
    x = product((backh[...], backl[...]), split(jnp.concatenate(turned, axis=1)))
    for m in range(2):
        signal[m : m + 1, :] = x[:, m * LANES : (m + 1) * LANES].reshape(1, LENGTH)
    sent[...] = signal[...].astype(BF)


def inverse(*args):
    return pl.pallas_call(
        inverse_kernel,
        out_shape=[jax.ShapeDtypeStruct((2, LENGTH), d) for d in (F32, BF)],
        compiler_params=params(12),
        name="inverse",
    )(*args)


def noise_kernel(place, modes, noise, plain, mirror, in_weight):
    high, low = split(jnp.dot(inward(place), local_modes(place, modes), precision=HI, preferred_element_type=F32).T)
    in_weight[...] = jnp.concatenate([high, low], axis=1)
    for m in range(2):
        n = noise[m].T
        r = lax.broadcasted_iota(jnp.int32, (ROWS, Q), 0)
        k = lax.broadcasted_iota(jnp.int32, (ROWS, Q), 1)
        rows = (k == ((Q - r) & (Q - 1))).astype(F32)
        a = lax.broadcasted_iota(jnp.int32, (LANES, LANES), 0)
        b = lax.broadcasted_iota(jnp.int32, (LANES, LANES), 1)
        turned = jnp.dot(jnp.dot(rows, n, precision=HI), (a + b == LANES - 1).astype(F32), precision=HI)
        first = lax.broadcasted_iota(jnp.int32, (ROWS, LANES), 0) == 0
        plain[m] = n[:ROWS]
        mirror[m] = jnp.where(first, n[:ROWS], turned)


def noise_tables(place, modes, noise):
    return pl.pallas_call(
        noise_kernel,
        out_shape=[jax.ShapeDtypeStruct((2, ROWS, LANES), F32)] * 2 + [jax.ShapeDtypeStruct((64, 128), BF)],
        in_specs=[pl.BlockSpec(memory_space=pltpu.SMEM), VMEM, VMEM],
        compiler_params=params(12),
        name="noise",
    )(place, modes, noise.reshape(2, LANES, Q))


def remove_kernel(weight, sky0, sky1, *refs):
    pieces, cleaned, out, sems = refs[:-3], refs[-3], refs[-2], refs[-1]
    copies = []
    for i in range(LENGTH // PIECE):
        at = pl.ds(i * PIECE, PIECE)
        which = int(i * PIECE >= FIRSTS[1])
        sky = (sky0, sky1)[which]
        signal = jnp.concatenate([p[:, at].astype(F32) for p in pieces], axis=0).astype(BF)
        fitted = jnp.dot(weight[...], jnp.concatenate([signal, signal], axis=0), preferred_element_type=F32)
        out[:, at] = (sky[:, pl.ds(i * PIECE - FIRSTS[which], PIECE)] - fitted).astype(BF)
        copies.append(pltpu.make_async_copy(out.at[:, at], cleaned.at[:, at], sems.at[i]))
        copies[-1].start()
    for copy in copies:
        copy.wait()


def remove(weight, skies, pieces):
    return pl.pallas_call(
        remove_kernel,
        out_shape=jax.ShapeDtypeStruct((64, LENGTH), BF),
        in_specs=[VMEM] * (3 + len(pieces)),
        out_specs=pl.BlockSpec(memory_space=HBM),
        scratch_shapes=[pltpu.VMEM((64, LENGTH), BF), pltpu.SemaphoreType.DMA((LENGTH // PIECE,))],
        compiler_params=params(24),
        name="remove",
    )(weight, *skies, *pieces)


def onward(x):
    return lax.ppermute(x, ("z", "c"), ONWARD)


def diagonal(x):
    return lax.ppermute(x, ("xl", "z", "c"), DIAGONAL)


def flip(x, axis):
    return lax.ppermute(x, axis, FLIP)


def reduced(far, own, oth):
    other = flip(oth, "c")
    got = onward(far)
    for hop in range(3):
        a = 8 * hop
        got = (own[a : a + 8] + other[a : a + 8] + got.astype(F32)).astype(BF)
        if hop < 2:
            got = onward(got)
    across = diagonal(got[4:])
    near = onward(got[:4])
    both = near.astype(F32) + across.astype(F32)
    return own[24:] + other[24:], both[:2], flip(both[2:], "c")


def over_dishes(power):
    here = power.astype(F32)
    for step in (1, 3, 2):
        moved = lax.ppermute(power, "y", [(i, (i + step) % 4) for i in range(4)])
        here = here + moved.astype(F32)
    return here, lax.ppermute(here.astype(BF), "xh", FLIP)


def gathered(quad, first):
    second = onward(first)
    third = onward(second)
    last = onward(third[:2])
    mine = [first, second, third]
    theirs = [flip(x, "c") for x in mine]
    return [quad] + mine + theirs + [last, flip(last, "c")]


def work(sky_data, eigenmodes, noise_power):
    xl, z, c = (lax.axis_index(n) for n in ("xl", "z", "c"))
    place = jnp.stack([xl * 8 + z, xl, z, c]).astype(jnp.int32)
    sky = sky_data[0]
    ahead, back = tables()
    out_weight, modes, *parts0 = project(place, None, pltpu.with_memory_space_constraint(eigenmodes.T, HBM), sky, 0)
    parts = [parts0, project(place, out_weight, None, sky, 1)]
    plain, mirror, in_weight = noise_tables(place, modes, noise_power)
    sums = [reduced(*p[1:]) for p in parts]
    beside = flip(jnp.concatenate([h[2:] for h, _, _ in sums], axis=1).astype(BF), "xl")
    totals = [
        home[:2] + both + beside[:, FIRSTS[i] : FIRSTS[i] + SPANS[i]].astype(F32) for i, (home, both, _) in enumerate(sums)
    ]
    real, imag, power = forward(totals, [c for _, _, c in sums], ahead)
    here, there = over_dishes(power)
    signal, sent = inverse(real, imag, here, there, plain, mirror, *back)
    quad = jnp.concatenate([sent, flip(sent, "c")])
    across = gathered(flip(quad, "xl"), diagonal(quad))
    near = gathered(quad, onward(quad))
    cleaned = remove(in_weight, [p[0] for p in parts], near + across)
    return cleaned[None], signal[None]


def solution(mesh):
    finer = Mesh(mesh.devices.reshape(4, 2, 2, 8, 2), ("y", "xh", "xl", "z", "c"))
    dish, blk = ("y", "xh"), ("xl", "z", "c")
    return jax.shard_map(
        work,
        mesh=finer,
        in_specs=(P(dish, blk, None), P(), P(blk, None)),
        out_specs=(P(dish, blk, None), P(dish, blk, None)),
        check_vma=False,
    )
```
